32 devices in a mesh: wave: 16 (over z, x, core), level: 2 (over y).
Axes of the slice: x: 2, y: 2, z: 4, core: 2. Of those that a mesh axis runs over, the one named last changes fastest.
Arguments:
- state: float32 [4, 64, 256, 2, 256], P(None, 'level', 'wave'), may hold values from -0.02 to 0.02
- legendre: float32 [256, 384, 256], P('wave'), may hold values from -6 to 6
- lat_weight: float32 [384], P('wave'), may hold values from 0.8 to 2
- modes: float32 [64, 64], replicated, may hold values from -1 to 1, as said below
- mode_rates: float32 [64], replicated, may hold values from 1e-05 to 0.003
- diffusion: float32 [4], replicated, may hold values from 0.3 to 3
- norm_gain: float32 [256], replicated, may hold values from 0.5 to 1.5
- w_first: bfloat16 [1024, 256], replicated, may hold values from -0.375 to 0.375
- b_first: float32 [1024], replicated, may hold values from -3 to 3
- w_second: bfloat16 [1024, 1024], replicated, may hold values from -0.1875 to 0.1875
- b_second: float32 [1024], replicated, may hold values from -3 to 3
- w_third: bfloat16 [256, 1024], replicated, may hold values from -0.1875 to 0.1875
- b_third: float32 [256], replicated, may hold values from -1.2 to 1.2
Outputs:
- next_state: float32 [4, 64, 256, 2, 256], P(None, 'level', 'wave')
The draws below stay inside these ranges and needn't reach their ends.
Inputs may be any that keep to these rules, and one draw needn't show every extreme that they name: `modes`: orthogonal: its transpose is its inverse.
All inputs are finite; a program needn't handle non-finite values.
Results may differ from the reference program's by a relative error of at most 0.0011.
Values may be sent and summed in bfloat16 or wider, within the bound.
A program may use at most 192 MiB of HBM per device.

```python
import math
import jax
import jax.numpy as jnp
from jax import lax

F = 4
LEV = 64
M = 256
LAT = 384
LON = 768
HID = 1024


def draw_modes(key, part):
    random_matrix = jax.random.normal(key, (LEV, LEV), jnp.float32)
    factors = jnp.linalg.qr(random_matrix)
    return factors[0].astype(jnp.float32)


def level_of(rng, extent, shards, least, largest):
    level, own = 1.0, jax.random.fold_in(rng, 6)
    for axis_at, shards_of in shards:
        heights = jnp.exp(jax.random.uniform(jax.random.fold_in(own, axis_at), (shards_of,), jnp.float32, least / len(shards), largest / len(shards)))
        level = level * jnp.repeat(heights, extent[axis_at] // shards_of).reshape([-1 if axis == axis_at else 1 for axis in range(len(extent))])
    return level


def gaussian(key, dims, deviation, bound, shards=(), kind=jnp.bfloat16):
    values = deviation * jax.random.normal(key, dims, jnp.float32)
    if shards:
        values = values * level_of(key, dims, shards, -0.22, 0.18)
    return jnp.clip(values, -bound, bound).astype(kind)


def setup_inputs(seed: int = 0) -> dict:
    key_of = jax.random.split(jax.random.key(seed), 14)
    state = gaussian(key_of[0], (F, LEV, M, 2, M), 0.003, 0.02, ((1, 2), (2, 16)), jnp.float32)
    legendre = gaussian(key_of[1], (M, LAT, M), 1.0, 6.0, ((0, 16),), jnp.float32)
    lat_weight = jnp.clip(0.8 + 1.2 * jax.random.uniform(key_of[2], (LAT,), jnp.float32) ** level_of(key_of[2], (LAT,), ((0, 16),), -0.2, 0.2), 0.8, 2.0)
    modes = draw_modes(jax.random.fold_in(key_of[13], 71), 0)
    mode_rates = jnp.clip(jnp.exp(jax.random.uniform(key_of[4], (LEV,), jnp.float32, math.log(9.999999747378752e-06), math.log(0.003))), 9.999999747378752e-06, 0.003)
    diffusion = jnp.clip(jnp.exp(jax.random.uniform(key_of[5], (F,), jnp.float32, math.log(0.3), math.log(3.0))), 0.3, 3.0)
    norm_gain = jnp.clip(1.0 + 0.1 * jax.random.normal(key_of[6], (F * LEV,), jnp.float32), 0.5, 1.5)
    w_first = gaussian(key_of[7], (HID, F * LEV), (F * LEV) ** -0.5, 0.375)
    b_first = gaussian(key_of[8], (HID,), 0.5, 3.0, (), jnp.float32)
    w_second = gaussian(key_of[9], (HID, HID), HID ** -0.5, 0.1875)
    b_second = gaussian(key_of[10], (HID,), 0.5, 3.0, (), jnp.float32)
    w_third = gaussian(key_of[11], (F * LEV, HID), HID ** -0.5, 0.1875)
    b_third = gaussian(key_of[12], (F * LEV,), 0.2, 1.2, (), jnp.float32)
    return dict(state=state, legendre=legendre, lat_weight=lat_weight, modes=modes, mode_rates=mode_rates, diffusion=diffusion, norm_gain=norm_gain, w_first=w_first, b_first=b_first, w_second=w_second, b_second=b_second, w_third=w_third, b_third=b_third)


highest = lax.Precision.HIGHEST
norm_eps = 1e-06

def phase_angles(waves, longitudes):
    wave_idx = jnp.arange(waves, dtype=jnp.int32)
    lon_idx = jnp.arange(longitudes, dtype=jnp.int32)
    phase_turns = wave_idx[:, None] * lon_idx[None, :] % longitudes
    return (2.0 * jnp.pi / longitudes * phase_turns.astype(jnp.float32), wave_idx)

def synthesis_table(waves, longitudes):
    angle_table, wave_idx = phase_angles(waves, longitudes)
    factor = jnp.where(wave_idx == 0, 1.0, 2.0).astype(jnp.float32)[:, None]
    return jnp.stack([factor * jnp.cos(angle_table), -factor * jnp.sin(angle_table)], axis=1)

def analysis_table(waves, longitudes):
    angle_table, wave_idx = phase_angles(waves, longitudes)
    flipped = angle_table.T
    return jnp.stack([jnp.cos(flipped), -jnp.sin(flipped)], axis=2) / longitudes

def column_physics(columns, norm_gain, w_first, b_first, w_second, b_second, w_third, b_third):
    values = columns.astype(jnp.float32)
    inverse_rms = lax.rsqrt(lax.optimization_barrier(jnp.mean(values * values, axis=0, keepdims=True)) + norm_eps)
    normed = (values * inverse_rms * norm_gain[:, None]).astype(jnp.bfloat16)
    hidden_one = jax.nn.gelu(jnp.dot(w_first.astype(jnp.float32), normed.astype(jnp.float32), preferred_element_type=jnp.float32) + b_first[:, None]).astype(jnp.bfloat16)
    hidden_two = jax.nn.gelu(jnp.dot(w_second.astype(jnp.float32), hidden_one.astype(jnp.float32), preferred_element_type=jnp.float32) + b_second[:, None]).astype(jnp.bfloat16)
    return (jnp.dot(w_third.astype(jnp.float32), hidden_two.astype(jnp.float32), preferred_element_type=jnp.float32) + b_third[:, None]).astype(jnp.bfloat16)

def reference(state, legendre, lat_weight, modes, mode_rates, diffusion, norm_gain, w_first, b_first, w_second, b_second, w_third, b_third):
    wave_idx = jnp.arange(M, dtype=jnp.int32)
    degree_index = wave_idx[:, None] + jnp.arange(M, dtype=jnp.int32)[None, :]
    kept_mask = (degree_index < M).astype(jnp.float32)
    kept_basis = legendre * kept_mask[:, None, :]
    band_coeffs = jnp.einsum('flmcj,maj->flmca', state, kept_basis, precision=highest)
    grid_field = jnp.einsum('flmca,mco->flao', band_coeffs, synthesis_table(M, LON), precision=highest)
    grid_low = grid_field.astype(jnp.bfloat16)

    def one_row(row_block):
        flat_cols = row_block.reshape(F * LEV, LON)
        return column_physics(flat_cols, norm_gain, w_first, b_first, w_second, b_second, w_third, b_third).reshape(F, LEV, LON)
    tendency = lax.map(one_row, jnp.moveaxis(grid_low, 2, 0))
    tendency = jnp.moveaxis(tendency, 0, 2)
    updated = (grid_field + tendency.astype(jnp.float32)) * lat_weight[None, None, :, None]
    wave_coeffs = jnp.einsum('flao,omc->flmca', updated, analysis_table(M, LON), precision=highest)
    spectral = jnp.einsum('flmca,maj->flmcj', wave_coeffs, kept_basis, precision=highest)
    growth = (degree_index * (degree_index + 1)).astype(jnp.float32)
    amplitude = jnp.einsum('lk,lmcj->kmcj', modes, spectral[1], precision=highest)
    amplitude = amplitude / (1.0 + mode_rates[:, None, None, None] * growth[None, :, None, :])
    solved = jnp.einsum('lk,kmcj->lmcj', modes, amplitude, precision=highest)
    combined = jnp.concatenate([spectral[:1], solved[None], spectral[2:]], axis=0)
    scaled_growth = growth / (M * (M - 1))
    damping = 1.0 + diffusion[:, None, None] * (scaled_growth * scaled_growth)[None]
    return combined / damping[:, None, :, None, :]
```

```python
import functools

import jax
import jax.numpy as jnp
from jax import lax
from jax.experimental import pallas as pl
from jax.experimental.pallas import tpu as pltpu
from jax.sharding import PartitionSpec as P

high = lax.Precision.HIGH
norm_eps = 1e-06
axes = ("wave", "level")
send_scale = 1024.0


def phase_angles(waves, longitudes):
    wave_idx = jnp.arange(waves, dtype=jnp.int32)
    lon_idx = jnp.arange(longitudes, dtype=jnp.int32)
    phase_turns = wave_idx[:, None] * lon_idx[None, :] % longitudes
    return (2.0 * jnp.pi / longitudes * phase_turns.astype(jnp.float32), wave_idx)


def synthesis_table(waves, longitudes):
    angle_table, wave_idx = phase_angles(waves, longitudes)
    factor = jnp.where(wave_idx == 0, 1.0, 2.0).astype(jnp.float32)[:, None]
    return jnp.stack([factor * jnp.cos(angle_table), -factor * jnp.sin(angle_table)], axis=1)


def analysis_table(waves, longitudes):
    angle_table, _ = phase_angles(waves, longitudes)
    return jnp.stack([jnp.cos(angle_table), -jnp.sin(angle_table)], axis=1) / longitudes


def contract_last(left, right):
    return lax.dot_general(
        left, right, (((1,), (1,)), ((), ())), preferred_element_type=jnp.float32
    )


def physics_kernel(grid_ref, lat_ref, gain_ref, w1_ref, b1_ref, w2_ref, b2_ref, w3_ref, b3_ref, out_ref, top_ref):
    grid_rows = grid_ref[0]
    values = grid_rows.astype(jnp.bfloat16).astype(jnp.float32)
    inverse_rms = lax.rsqrt(jnp.mean(values * values, axis=1, keepdims=True) + norm_eps)
    normed = (values * inverse_rms * gain_ref[...]).astype(jnp.bfloat16)
    hidden = jax.nn.gelu(contract_last(normed, w1_ref[...]) + b1_ref[...]).astype(jnp.bfloat16)
    hidden = jax.nn.gelu(contract_last(hidden, w2_ref[...]) + b2_ref[...]).astype(jnp.bfloat16)
    tendency = (contract_last(hidden, w3_ref[...]) + b3_ref[...]).astype(jnp.bfloat16)
    updated = (grid_rows + tendency.astype(jnp.float32)) * lat_ref[pl.program_id(0)]
    out_ref[0] = updated
    top_ref[0] = jnp.max(jnp.abs(updated), axis=0, keepdims=True)


def column_step(grid, lat, gain, w1, b1, w2, b2, w3, b3):
    rows, lon, feats = grid.shape
    hid = w1.shape[0]
    whole = lambda *shape: pl.BlockSpec(shape, lambda i: (0,) * len(shape))
    block = pl.BlockSpec((1, lon, feats), lambda i: (i, 0, 0))
    return pl.pallas_call(
        physics_kernel,
        grid=(rows,),
        out_shape=(
            jax.ShapeDtypeStruct((rows, lon, feats), jnp.float32),
            jax.ShapeDtypeStruct((rows, 1, feats), jnp.float32),
        ),
        in_specs=[
            block,
            pl.BlockSpec(memory_space=pltpu.SMEM),
            whole(1, feats),
            whole(hid, feats),
            whole(1, hid),
            whole(hid, hid),
            whole(1, hid),
            whole(feats, hid),
            whole(1, feats),
        ],
        out_specs=(block, pl.BlockSpec((1, 1, feats), lambda i: (i, 0, 0))),
        compiler_params=pltpu.CompilerParams(vmem_limit_bytes=56 * 1024 * 1024),
    )(grid, lat, gain[None], w1, b1[None], w2, b2[None], w3, b3[None])


def body(
    longitudes,
    state,
    legendre,
    lat_weight,
    modes,
    mode_rates,
    diffusion,
    norm_gain,
    w_first,
    b_first,
    w_second,
    b_second,
    w_third,
    b_third,
):
    fields, lev_dev, m_dev, parts, degrees = state.shape
    levels = modes.shape[0]
    waves = degrees
    wave_count = lax.axis_size("wave")
    level_count = lax.axis_size("level")
    lat_band = lat_weight.shape[0]
    lat_own = -(-lat_band // level_count)
    lat_extra = lat_own * level_count - lat_band
    wave_global = lax.axis_index("wave") * m_dev + jnp.arange(m_dev, dtype=jnp.int32)
    degree_index = wave_global[:, None] + jnp.arange(degrees, dtype=jnp.int32)[None, :]
    kept_mask = (degree_index < waves).astype(jnp.float32)
    basis = legendre * kept_mask[:, None, :]
    if lat_extra:
        basis = basis.reshape(m_dev, wave_count, lat_band, degrees)
        basis = jnp.pad(basis, ((0, 0), (0, 0), (0, lat_extra), (0, 0)))
        basis = basis.reshape(m_dev, -1, degrees)
        lat_weight = jnp.pad(lat_weight, (0, lat_extra))
    inverse_tab = synthesis_table(waves, longitudes).reshape(wave_count, m_dev, parts, longitudes)
    forward_tab = analysis_table(waves, longitudes).reshape(wave_count, m_dev, parts, longitudes)

    band = jnp.einsum("flmcj,maj->amcfl", state, basis, precision=high)
    band = (band * send_scale).astype(jnp.float16)
    band = band.reshape(wave_count * level_count, lat_own, m_dev, parts, fields, lev_dev)
    band = lax.all_to_all(band, axes, split_axis=0, concat_axis=0, tiled=True)
    band = band.reshape(wave_count, level_count, lat_own, m_dev, parts, fields, lev_dev)
    band = band.astype(jnp.float32) * (1.0 / send_scale)
    grid = jnp.einsum("wvamcfl,wmco->aovfl", band, inverse_tab, precision=high)
    feats = fields * levels
    grid = grid.reshape(lat_own, longitudes, feats)

    def slabs_first(x):
        split = x.reshape((fields, level_count, lev_dev) + x.shape[1:])
        return jnp.swapaxes(split, 0, 1).reshape(x.shape)

    lat = lax.dynamic_slice_in_dim(lat_weight, lax.axis_index("level") * lat_own, lat_own, 0)
    updated, tops = column_step(
        grid,
        lat,
        slabs_first(norm_gain),
        slabs_first(w_first.T).T,
        b_first,
        w_second,
        b_second,
        slabs_first(w_third),
        slabs_first(b_third),
    )
    top = jnp.maximum(jnp.max(tops), 1e-25)
    reach = 32768.0 / levels**0.5
    tops_all = lax.all_gather(top / reach, axes).reshape(wave_count, level_count)

    wave = jnp.einsum("aok,wmco->wmcak", updated, forward_tab, precision=high)
    wave = wave * (reach / top)
    wave = wave.reshape(wave_count, m_dev, parts, lat_own, level_count, fields, lev_dev)
    modal = jnp.einsum(
        "wmcavl,vlk->wmcak",
        wave[..., 1, :],
        modes.reshape(level_count, lev_dev, levels),
        precision=high,
    )
    others = jnp.concatenate([wave[..., :1, :], wave[..., 2:, :]], axis=-2)
    others = others.reshape(wave_count, m_dev, parts, lat_own, level_count, (fields - 1) * lev_dev)
    others = jnp.moveaxis(others, 4, 1)
    modal = jnp.broadcast_to(modal[:, None], others.shape[:-1] + (levels,))
    sent = jnp.concatenate([others, modal], axis=-1).astype(jnp.float16)
    sent = sent.reshape((wave_count * level_count,) + sent.shape[2:])
    got = lax.all_to_all(sent, axes, split_axis=0, concat_axis=0, tiled=True)
    got = got.reshape((wave_count, level_count) + got.shape[1:]).astype(jnp.float32)
    got = got * tops_all[:, :, None, None, None, None]
    basis_split = basis.reshape(m_dev, wave_count, level_count, lat_own, degrees)
    spectral = jnp.einsum("wvmcaq,mwvaj->qmcj", got, basis_split, precision=high)

    growth = (degree_index * (degree_index + 1)).astype(jnp.float32)
    plain = spectral[: (fields - 1) * lev_dev].reshape(fields - 1, lev_dev, m_dev, parts, degrees)
    divisor = 1.0 + mode_rates[:, None, None, None] * growth[None, :, None, :]
    amplitude = spectral[(fields - 1) * lev_dev :] / divisor
    own_rows = lax.dynamic_slice_in_dim(modes, lax.axis_index("level") * lev_dev, lev_dev, 0)
    solved = jnp.einsum("lk,kmcj->lmcj", own_rows, amplitude, precision=high)
    combined = jnp.concatenate([plain[:1], solved[None], plain[1:]], axis=0)
    scaled_growth = growth / (waves * (waves - 1))
    damping = 1.0 + diffusion[:, None, None] * (scaled_growth * scaled_growth)[None]
    return combined / damping[:, None, :, None, :]


def solution(mesh):
    def step(state, legendre, *rest):
        longitudes = 2 * legendre.shape[1]
        mapped = jax.shard_map(
            functools.partial(body, longitudes),
            mesh=mesh,
            in_specs=(P(None, "level", "wave", None, None), P("wave", None, None), P("wave")) + (P(),) * 10,
            out_specs=P(None, "level", "wave", None, None),
            check_vma=False,
        )
        return mapped(state, legendre, *rest)

    return step
```
